512 devices in a mesh: head: 8 (over y, core), seq: 64 (over z, x).
Axes of the slice: x: 4, y: 4, z: 16, core: 2. Of those that a mesh axis runs over, the one named last changes fastest.
Arguments:
- queries: bfloat16 [16384, 4096], P('seq', 'head'), may hold values from -6 to 6
- keys: bfloat16 [16384, 4096], P('seq', 'head'), may hold values from -6 to 6
- values: bfloat16 [16384, 4096], P('seq', 'head'), may hold values from -6 to 6
- token_rates: float32 [16, 16384], P('head', 'seq'), may hold values from 0.05 to 1
- w_gate: bfloat16 [16, 256, 512], P('head'), may hold values from -6 to 6
- w_up: bfloat16 [16, 256, 512], P('head'), may hold values from -6 to 6
- w_down: bfloat16 [16, 512, 256], P('head'), may hold values from -6 to 6
Outputs:
- applied: bfloat16 [16384, 4096], P('seq', 'head')
- step_gate: bfloat16 [16, 256, 512], P('head')
- step_up: bfloat16 [16, 256, 512], P('head')
- step_down: bfloat16 [16, 256, 512], P('head')
The draws below stay inside these ranges and needn't reach their ends.
All inputs are finite; a program needn't handle non-finite values.
Results may differ from the reference program's by a relative error of at most 0.035.
Values may be sent and summed in bfloat16 or wider, within the bound.
A program may use at most 64 MiB of HBM per device.

```python
import math
import jax
import jax.numpy as jnp

HEADS = 16
DH = 256
HID = 512
NS_STEPS = 5
SEQ_LEN = 16384


def steps_of(own_key, dims, split, least, largest):
    loudness, own = 1.0, jax.random.fold_in(own_key, 6)
    for axis_at, shards_of in split:
        heights = jnp.exp(jax.random.uniform(jax.random.fold_in(own, axis_at), (shards_of,), jnp.float32, least / len(split), largest / len(split)))
        loudness = loudness * jnp.repeat(heights, dims[axis_at] // shards_of).reshape([-1 if axis == axis_at else 1 for axis in range(len(dims))])
    return loudness


def centred(rng, dims, width, bound, shards=(), held_as=jnp.bfloat16):
    factor_of = steps_of(rng, dims, shards, -0.22, 0.18) if shards else 1.0
    values = jax.random.normal(rng, dims, jnp.float32) * width * factor_of
    return jnp.minimum(jnp.maximum(values, -bound), bound).astype(held_as)


def setup_inputs(seed: int = 0) -> dict:
    splits = jax.random.split(jax.random.key(seed), 8)
    return {
        "queries": centred(splits[0], (SEQ_LEN, HEADS * DH), 1.0, 6.0, ((0, 64), (1, 8))),
        "keys": centred(splits[1], (SEQ_LEN, HEADS * DH), 1.0, 6.0, ((0, 64), (1, 8))),
        "values": centred(splits[2], (SEQ_LEN, HEADS * DH), 1.0, 6.0, ((0, 64), (1, 8))),
        "token_rates": jnp.clip(jnp.exp(math.log(1.0) - 2.9957323 * jax.random.uniform(splits[3], (HEADS, SEQ_LEN), jnp.float32) ** steps_of(splits[3], (HEADS, SEQ_LEN), ((0, 8), (1, 64)), -0.2, 0.2)), 0.05, 1.0),
        "w_gate": centred(splits[4], (HEADS, DH, HID), 1.0, 6.0, ((0, 8),)),
        "w_up": centred(splits[5], (HEADS, DH, HID), 1.0, 6.0, ((0, 8),)),
        "w_down": centred(splits[6], (HEADS, HID, DH), 1.0, 6.0, ((0, 8),)),
    }


def newton(grad):
    norm = jnp.sqrt(jnp.sum(grad * grad))
    xmat = (grad / (norm + 1e-07)).astype(jnp.bfloat16)
    for step in range(NS_STEPS):
        amat = jnp.dot(xmat, xmat.T, preferred_element_type=jnp.float32).astype(jnp.bfloat16)
        bmat = (-4.775 * amat.astype(jnp.float32) + 2.0315 * jnp.dot(amat, amat, preferred_element_type=jnp.float32)).astype(jnp.bfloat16)
        nxt = 3.4445 * xmat.astype(jnp.float32) + jnp.dot(bmat, xmat, preferred_element_type=jnp.float32)
        if step == NS_STEPS - 1:
            nxt = nxt * (0.2 * math.sqrt(HID))
        xmat = nxt.astype(jnp.bfloat16)
    return xmat

def reference(queries, keys, values, token_rates, w_gate, w_up, w_down):
    scale_one = DH ** (-0.5)
    scale_two = HID ** (-0.5)
    outs_list, gate_list, up_list, down_list = ([], [], [], [])
    for head in range(HEADS):
        cols = slice(head * DH, (head + 1) * DH)
        qpart, kpart, vpart = (queries[:, cols], keys[:, cols], values[:, cols])
        gq = scale_one * jnp.dot(qpart, w_gate[head], preferred_element_type=jnp.float32)
        uq = scale_one * jnp.dot(qpart, w_up[head], preferred_element_type=jnp.float32)
        hq = (jax.nn.silu(gq) * uq).astype(jnp.bfloat16)
        outs_list.append((scale_two * jnp.dot(hq, w_down[head], preferred_element_type=jnp.float32)).astype(jnp.bfloat16))
        gk = scale_one * jnp.dot(kpart, w_gate[head], preferred_element_type=jnp.float32)
        uk = scale_one * jnp.dot(kpart, w_up[head], preferred_element_type=jnp.float32)
        hk = (jax.nn.silu(gk) * uk).astype(jnp.bfloat16)
        vrate = (token_rates[head][:, None] * vpart.astype(jnp.float32)).astype(jnp.bfloat16)
        gdown = -scale_two * jnp.dot(vrate.T, hk, preferred_element_type=jnp.float32)
        dhid = -scale_two * jnp.dot(vrate, w_down[head].T, preferred_element_type=jnp.float32)
        sig = jax.nn.sigmoid(gk)
        dgate = (dhid * uk * sig * (1.0 + gk * (1.0 - sig))).astype(jnp.bfloat16)
        dup = (dhid * jax.nn.silu(gk)).astype(jnp.bfloat16)
        ggate = scale_one * jnp.dot(kpart.T, dgate, preferred_element_type=jnp.float32)
        gup = scale_one * jnp.dot(kpart.T, dup, preferred_element_type=jnp.float32)
        gate_list.append(newton(ggate))
        up_list.append(newton(gup))
        down_list.append(newton(gdown))
    return (jnp.concatenate(outs_list, axis=1), jnp.stack(gate_list), jnp.stack(up_list), jnp.stack(down_list))
```

```python
import math

import jax
import jax.numpy as jnp
from jax import lax
from jax.experimental import pallas as pl
from jax.experimental.pallas import tpu as pltpu
from jax.sharding import PartitionSpec as P

NS_STEPS = 5
NX = 4
NZ = 16
GROUPS = 3
PER = 2
F32 = jnp.float32
BF16 = jnp.bfloat16
MESH = pl.DeviceIdType.MESH


def dot(a, b, ca, cb):
    return lax.dot_general(a, b, (((ca,), (cb,)), ((), ())), preferred_element_type=F32)


def sigmoid(x):
    return 0.5 * jnp.tanh(0.5 * x) + 0.5


def slot_of(head, kind):
    if kind == 2:
        return 0, head
    return 1 + head, kind


def grads_kernel(q_ref, k_ref, v_ref, r_ref, wg_ref, wu_ref, wd_ref, app_ref, g_ref):
    heads, dh, hid = wg_ref.shape
    s1, s2 = dh ** (-0.5), hid ** (-0.5)
    rates = jnp.transpose(r_ref[...])
    half = hid // 2
    for h in range(heads):
        cols = slice(h * dh, (h + 1) * dh)
        q, k = q_ref[:, cols], k_ref[:, cols]
        vr = (rates[:, h : h + 1] * v_ref[:, cols].astype(F32)).astype(BF16)
        kt = jnp.transpose(k)
        vt = jnp.transpose(vr)
        acc = None
        for j in range(2):
            js = slice(j * half, (j + 1) * half)
            wg, wu, wd = wg_ref[h, :, js], wu_ref[h, :, js], wd_ref[h, js, :]
            gk = s1 * dot(k, wg, 1, 0)
            uk = s1 * dot(k, wu, 1, 0)
            dhid = -s2 * dot(vr, wd, 1, 1)
            sig = sigmoid(gk)
            silu = gk * sig
            hk = (silu * uk).astype(BF16)
            dg = (dhid * uk * (sig * (1.0 + gk * (1.0 - sig)))).astype(BF16)
            du = (dhid * silu).astype(BF16)
            for kind, lhs, rhs, scale in ((2, vt, hk, -s2), (0, kt, dg, s1), (1, kt, du, s1)):
                out = (scale * dot(lhs, rhs, 1, 0)).astype(BF16)
                group, place = slot_of(h, kind)
                for c in range(2):
                    g_ref[group, 2 * j + c, place] = out[:, c * 128 : (c + 1) * 128]
            gq = s1 * dot(q, wg, 1, 0)
            uq = s1 * dot(q, wu, 1, 0)
            hq = (gq * sigmoid(gq) * uq).astype(BF16)
            part = dot(hq, wd, 1, 0)
            acc = part if acc is None else acc + part
        app_ref[:, cols] = (s2 * acc).astype(BF16)


def wait_all(ref, sem):
    pltpu.make_async_copy(ref, ref, sem).wait()


def reduce_kernel(g_ref, o_ref, xr, zs, zr, sems):
    me = lax.axis_index("seq")
    z, x = me // NX, me % NX

    def along_x(d):
        return z * NX + (x + d) % NX

    def along_z(d):
        return ((z + d) % NZ) * NX + x

    def send(src, dst, kind, group, peer):
        pltpu.make_async_remote_copy(
            src_ref=src,
            dst_ref=dst,
            send_sem=sems.at[kind, group],
            recv_sem=sems.at[4 + kind, group],
            device_id={"seq": peer},
            device_id_type=MESH,
        ).start()

    barrier = pltpu.get_barrier_semaphore()
    for d in range(1, NX):
        pl.semaphore_signal(barrier, inc=1, device_id={"seq": along_x(d)}, device_id_type=MESH)
    for d in range(1, NZ):
        pl.semaphore_signal(barrier, inc=1, device_id={"seq": along_z(d)}, device_id_type=MESH)
    pl.semaphore_wait(barrier, NX + NZ - 2)

    mine = pl.ds(pl.multiple_of(z * 16, 16), 16)
    for g in range(GROUPS):
        for d in (2, 1, 3):
            send(g_ref.at[g, (x + d) % NX], xr.at[g, d - 1], 0, g, along_x(d))
    for g in range(GROUPS):
        wait_all(xr.at[g], sems.at[4, g])
        total = g_ref[g, x].astype(F32)
        for d in range(NX - 1):
            total = total + xr[g, d].astype(F32)
        zs[g] = total.astype(BF16)
        for d in (8, 7, 9, 6, 10, 5, 11, 4, 12, 3, 13, 2, 14, 1, 15):
            theirs = pl.ds(pl.multiple_of(((z + d) % NZ) * 16, 16), 16)
            send(zs.at[g, :, theirs], zr.at[g, d - 1], 1, g, along_z(d))
    for g in range(GROUPS):
        wait_all(zr.at[g], sems.at[5, g])
        total = zs[g, :, mine].astype(F32)
        for d in range(NZ - 1):
            total = total + zr[g, d].astype(F32)
        o_ref[g, x, :, mine] = total.astype(BF16)
        for d in (8, 7, 9, 6, 10, 5, 11, 4, 12, 3, 13, 2, 14, 1, 15):
            chunk = o_ref.at[g, x, :, mine]
            send(chunk, chunk, 2, g, along_z(d))
    for g in range(GROUPS):
        wait_all(zr.at[g], sems.at[6, g])
        for d in (2, 1, 3):
            send(o_ref.at[g, x], o_ref.at[g, x], 3, g, along_x(d))
    for g in range(GROUPS):
        wait_all(xr.at[g], sems.at[7, g])
    for g in range(GROUPS):
        wait_all(xr.at[g], sems.at[0, g])
        wait_all(zr.at[g], sems.at[1, g])
        wait_all(zr.at[g], sems.at[2, g])
        wait_all(xr.at[g], sems.at[3, g])


def newton_kernel(t_ref, gate_ref, up_ref, down_ref, x_ref):
    outs = (gate_ref, up_ref, down_ref)
    heads, _, hid = gate_ref.shape
    where = [(h, kind) for h in range(heads) for kind in (2, 0, 1)]
    for m, (h, kind) in enumerate(where):
        group, place = slot_of(h, kind)
        total = jnp.concatenate(
            [t_ref[group, c, place].astype(F32) for c in range(NX)], axis=1
        )
        norm = jnp.sqrt(jnp.sum(total * total, keepdims=True)) + 1e-07
        x_ref[m] = (total / norm).astype(BF16)

    def step(s, carry):
        scale = jnp.where(s == NS_STEPS - 1, 0.2 * math.sqrt(hid), 1.0).astype(F32)
        for m in range(len(where)):
            x = x_ref[m]
            a = dot(x, x, 1, 1).astype(BF16)
            b = (-4.775 * a.astype(F32) + 2.0315 * dot(a, a, 1, 0)).astype(BF16)
            nxt = 3.4445 * x.astype(F32) + dot(b, x, 1, 0)
            x_ref[m] = (nxt * scale).astype(BF16)
        return carry

    lax.fori_loop(0, NS_STEPS, step, 0)
    for m, (h, kind) in enumerate(where):
        outs[kind][h] = x_ref[m]


def per_device(queries, keys, values, token_rates, w_gate, w_up, w_down):
    heads, dh, hid = w_gate.shape
    tokens = queries.shape[0]
    vmem = pl.BlockSpec(memory_space=pltpu.VMEM)
    travel = jax.ShapeDtypeStruct((GROUPS, NX, PER, dh, hid // NX), BF16)
    applied, grads = pl.pallas_call(
        grads_kernel,
        name="grads",
        out_shape=(jax.ShapeDtypeStruct((tokens, heads * dh), BF16), travel),
        in_specs=[vmem] * 7,
        out_specs=(vmem, vmem),
        compiler_params=pltpu.CompilerParams(vmem_limit_bytes=24 << 20),
    )(queries, keys, values, token_rates, w_gate, w_up, w_down)
    total = pl.pallas_call(
        reduce_kernel,
        name="reduce",
        out_shape=travel,
        in_specs=[vmem],
        out_specs=vmem,
        scratch_shapes=[
            pltpu.VMEM((GROUPS, NX - 1, PER, dh, hid // NX), BF16),
            pltpu.VMEM((GROUPS, PER, dh, hid // NX), BF16),
            pltpu.VMEM((GROUPS, NZ - 1, PER, dh // NZ, hid // NX), BF16),
            pltpu.SemaphoreType.DMA((8, GROUPS)),
        ],
        compiler_params=pltpu.CompilerParams(
            collective_id=0, has_side_effects=True, vmem_limit_bytes=24 << 20
        ),
    )(grads)
    weights = jax.ShapeDtypeStruct((heads, dh, hid), BF16)
    gate, up, down = pl.pallas_call(
        newton_kernel,
        name="newton",
        out_shape=(weights,) * 3,
        in_specs=[vmem],
        out_specs=(vmem,) * 3,
        scratch_shapes=[pltpu.VMEM((heads * 3, dh, hid), BF16)],
        compiler_params=pltpu.CompilerParams(vmem_limit_bytes=24 << 20),
    )(total)
    return (applied, gate, up, down)


def solution(mesh):
    in_specs = (
        P("seq", "head"),
        P("seq", "head"),
        P("seq", "head"),
        P("head", "seq"),
        P("head", None, None),
        P("head", None, None),
        P("head", None, None),
    )
    out_specs = (
        P("seq", "head"),
        P("head", None, None),
        P("head", None, None),
        P("head", None, None),
    )
    return jax.shard_map(
        per_device, mesh=mesh, in_specs=in_specs, out_specs=out_specs, check_vma=False
    )
```

```python
import math

import jax
import jax.numpy as jnp
from jax import lax
from jax.experimental import pallas as pl
from jax.experimental.pallas import tpu as pltpu
from jax.sharding import PartitionSpec as P

NS_STEPS = 5
NX = 4
NZ = 16
GROUPS = 3
PER = 2
F32 = jnp.float32
BF16 = jnp.bfloat16
MESH = pl.DeviceIdType.MESH


def dot(a, b, ca, cb):
    return lax.dot_general(a, b, (((ca,), (cb,)), ((), ())), preferred_element_type=F32)


def sigmoid(x):
    return 0.5 * jnp.tanh(0.5 * x) + 0.5


def wait_all(ref, sem):
    pltpu.make_async_copy(ref, ref, sem).wait()


def token_grads(k, vr, wg, wu, wd, s1, s2):
    gk = s1 * dot(k, wg, 1, 0)
    uk = s1 * dot(k, wu, 1, 0)
    dhid = -s2 * dot(vr, wd, 1, 1)
    sig = sigmoid(gk)
    silu = gk * sig
    hk = (silu * uk).astype(BF16)
    dg = (dhid * uk * (sig * (1.0 + gk * (1.0 - sig)))).astype(BF16)
    du = (dhid * silu).astype(BF16)
    kt = jnp.transpose(k)
    return (
        -s2 * dot(jnp.transpose(vr), hk, 1, 0),
        s1 * dot(kt, dg, 1, 0),
        s1 * dot(kt, du, 1, 0),
    )


def head_apply(h, q, wg, wu, wd):
    dh, hid = wg.shape[1:]
    s1, s2 = dh ** (-0.5), hid ** (-0.5)
    half = hid // 2
    total = None
    for j in range(2):
        js = slice(j * half, (j + 1) * half)
        gq = s1 * dot(q, wg[h, :, js], 1, 0)
        uq = s1 * dot(q, wu[h, :, js], 1, 0)
        hq = (gq * sigmoid(gq) * uq).astype(BF16)
        part = dot(hq, wd[h, js, :], 1, 0)
        total = part if total is None else total + part
    return (s2 * total).astype(BF16)


TOKENS, NEAR, FAR, SPREAD, FILL, SIDE, PASS = range(7)
KINDS = 7
STRIDE = 5
STEPS = (1, 2, -1, -2)
LATENCY, INTERVAL = 3.0, 1.0


def main_kernel(
    q_hbm, k_hbm, v_hbm, r_hbm, wg_hbm, wu_hbm, wd_hbm, app_ref, o_ref,
    q_ref, k_ref, v_ref, r_ref, wg, wu, wd, wg_own, wu_own, wd_own, kv, acc, own,
    near, got, far, spread, loads, sems,
):
    heads, dh, hid = wg.shape
    s1, s2 = dh ** (-0.5), hid ** (-0.5)
    me = lax.axis_index("seq")
    z, x = me // NX, me % NX
    right, left_x = (x + 1) % NX, (x + NX - 1) % NX
    split = NX // heads
    own_head = x // split
    part = pl.ds(pl.multiple_of((x % split) * (hid // split), hid // split), hid // split)

    def along_x(d):
        return z * NX + (x + d) % NX

    def along_z(d):
        return ((z + d) % NZ) * NX + x

    def send(src, dst, kind, group, peer):
        pltpu.make_async_remote_copy(
            src_ref=src,
            dst_ref=dst,
            send_sem=sems.at[kind, group],
            recv_sem=sems.at[KINDS + kind, group],
            device_id={"seq": peer},
            device_id_type=MESH,
        ).start()

    def arrived(ref, kind, group):
        wait_all(ref, sems.at[KINDS + kind, group])

    def left(ref, kind, group):
        wait_all(ref, sems.at[kind, group])

    def rows(d):
        return pl.ds(pl.multiple_of(((z + d) % NZ) * 16, 16), 16)

    copies = [(r_hbm, r_ref), (v_hbm, v_ref)]
    copies += [(k_hbm.at[:, pl.ds(h * dh, dh)], k_ref.at[0, h]) for h in range(heads)]
    copies += [
        (wg_hbm.at[own_head, :, part], wg_own),
        (wu_hbm.at[own_head, :, part], wu_own),
        (wd_hbm.at[own_head, part], wd_own),
        (q_hbm, q_ref),
        (wg_hbm, wg),
        (wu_hbm, wu),
        (wd_hbm, wd),
    ]
    copies = [pltpu.make_async_copy(a, b, loads.at[i]) for i, (a, b) in enumerate(copies)]
    for copy in copies:
        copy.start()
    barrier = pltpu.get_barrier_semaphore()
    peers = [along_x(d) for d in (1, 2, 3)]
    peers += [along_z(d) for d in (1, -1, 2, -2, 3, -3, 5, -5)]
    for peer in peers:
        pl.semaphore_signal(barrier, inc=1, device_id={"seq": peer}, device_id_type=MESH)

    def start_z(g):
        def chunk(d):
            return own[g, :, rows(d)]

        for j, t in enumerate(STEPS):
            for i in range(3):
                near[g, 3 * j + i] = chunk(t + STRIDE * (i - 1))
            send(near.at[g, pl.ds(3 * j, 3)], got.at[g, pl.ds(3 * j, 3)], NEAR, g, along_z(t))
        near[g, 12] = chunk(-8)
        send(near.at[g, 12], got.at[g, 12], NEAR, g, along_z(-3))
        for i in range(3):
            near[g, 13 + i] = chunk(STRIDE * (i - 1))

    def collect(g):
        arrived(got.at[g], NEAR, g)
        for i in (0, 2, 1):
            total = near[g, 13 + i].astype(F32)
            for j in range(4):
                total = total + got[g, 3 * j + i].astype(F32)
            if i == 0:
                total = total + got[g, 12].astype(F32)
            near[g, 13 + i] = total.astype(BF16)
            if i != 1:
                send(near.at[g, 13 + i], far.at[g, i // 2], FAR, g, along_z(STRIDE * (i - 1)))

    def finish_sum(g):
        arrived(far.at[g], FAR, g)
        total = near[g, 14].astype(F32) + far[g, 0].astype(F32) + far[g, 1].astype(F32)
        spread[g, 1] = total.astype(BF16)
        send(spread.at[g, 1], spread.at[g, 2], SPREAD, g, along_z(-STRIDE))
        send(spread.at[g, 1], spread.at[g, 0], SPREAD, g, along_z(STRIDE))

    def fill(g):
        arrived(far.at[g], SPREAD, g)
        for j, t in enumerate(STEPS):
            mine = spread.at[g, pl.ds(0, 3)]
            send(mine, spread.at[g, pl.ds(3 + 3 * j, 3)], FILL, g, along_z(t))
        send(spread.at[g, 0], spread.at[g, 15], FILL, g, along_z(3))

    def side(g):
        arrived(got.at[g], FILL, g)
        for j, t in enumerate((0,) + STEPS):
            for i in range(3):
                o_ref[g, x, :, rows(STRIDE * (i - 1) - t)] = spread[g, 3 * j + i]
        o_ref[g, x, :, rows(8)] = spread[g, 15]
        for d in (1, -1):
            send(o_ref.at[g, x], o_ref.at[g, x], SIDE, g, along_x(d))

    def pass_on(g):
        arrived(o_ref.at[g, pl.ds(0, 2)], SIDE, g)
        send(o_ref.at[g, left_x, 0], o_ref.at[g, left_x, 0], PASS, g, along_x(1))
        send(o_ref.at[g, right, 1], o_ref.at[g, right, 1], PASS, g, along_x(-1))

    def end(g):
        arrived(o_ref.at[g, 0], PASS, g)

    for copy in copies[: 2 + heads]:
        copy.wait()
    rates = jnp.transpose(r_ref[...])
    for h in range(heads):
        v = v_ref[:, h * dh : (h + 1) * dh].astype(F32)
        k_ref[1, h] = (rates[:, h : h + 1] * v).astype(BF16)
    pl.semaphore_wait(barrier, len(peers))
    for i in range(2):
        for d in (2, 1, 3):
            theirs = k_ref.at[i, (x + d) % NX // split]
            send(theirs, kv.at[d - 1, i], TOKENS, d - 1, along_x(d))
    for copy in copies[2 + heads : 5 + heads]:
        copy.wait()
    weights = (wg_own[...], wu_own[...], wd_own[...], s1, s2)
    for g, grad in enumerate(token_grads(k_ref[0, own_head], k_ref[1, own_head], *weights)):
        acc[g] = grad
    for copy in copies[5 + heads :]:
        copy.wait()
    for h in range(heads):
        cols = slice(h * dh, (h + 1) * dh)
        app_ref[:, cols] = head_apply(h, q_ref[:, cols], wg, wu, wd)
    for d in (1, 3):
        arrived(kv.at[d - 1], TOKENS, d - 1)
        for g, grad in enumerate(token_grads(kv[d - 1, 0], kv[d - 1, 1], *weights)):
            acc[g] = acc[g] + grad
    arrived(kv.at[1], TOKENS, 1)
    for g, grad in enumerate(token_grads(kv[1, 0], kv[1, 1], *weights)):
        total = (acc[g] + grad).astype(BF16)
        for c in range(PER):
            own[g, c] = total[:, c * 128 : (c + 1) * 128]
        start_z(g)
    stages = (collect, finish_sum, fill, side, pass_on, end)
    order = sorted(
        (LATENCY * s + INTERVAL * g, s, g) for s in range(len(stages)) for g in range(GROUPS)
    )
    for _, s, g in order:
        stages[s](g)
    for g in range(GROUPS):
        left(kv.at[g], TOKENS, g)
        left(got.at[g], NEAR, g)
        left(far.at[g], FAR, g)
        left(far.at[g], SPREAD, g)
        left(got.at[g], FILL, g)
        left(o_ref.at[g, pl.ds(0, 2)], SIDE, g)
        left(o_ref.at[g, 0], PASS, g)


def newton_kernel(
    t_ref, applied_ref, applied_hbm, gate_hbm, up_hbm, down_hbm, x_ref, a_ref, sems
):
    outs = (gate_hbm, up_hbm, down_hbm)
    heads, _, hid = gate_hbm.shape
    handed = pltpu.make_async_copy(applied_ref, applied_hbm, sems.at[heads * 3])
    handed.start()
    where = [(h, kind) for h in range(heads) for kind in (2, 0, 1)]
    for m, (h, kind) in enumerate(where):
        blocks = [divmod(i, PER) for i in range(hid // 128)]
        split = NX // heads
        total = jnp.concatenate(
            [t_ref[(kind + 1) % 3, split * h + c, i].astype(F32) for c, i in blocks], axis=1
        )
        norm = jnp.sqrt(jnp.sum(total * total, keepdims=True)) + 1e-07
        x_ref[m] = (total / norm).astype(BF16)

    for s in range(NS_STEPS):
        for m in range(len(where)):
            x = x_ref[m]
            a_ref[m] = dot(x, x, 1, 1).astype(BF16)
        for m in range(len(where)):
            a = a_ref[m]
            b = -4.775 * a.astype(F32) + 2.0315 * dot(a, a, 1, 0)
            a_ref[m] = b.astype(BF16)
        for m in range(len(where)):
            x = x_ref[m]
            nxt = 3.4445 * x.astype(F32) + dot(a_ref[m], x, 1, 0)
            if s == NS_STEPS - 1:
                nxt = nxt * (0.2 * math.sqrt(hid))
            x_ref[m] = nxt.astype(BF16)
            if s == NS_STEPS - 1:
                h, kind = where[m]
                pltpu.make_async_copy(x_ref.at[m], outs[kind].at[h], sems.at[m]).start()
    for m, (h, kind) in enumerate(where):
        pltpu.make_async_copy(x_ref.at[m], outs[kind].at[h], sems.at[m]).wait()
    handed.wait()


def per_device(queries, keys, values, token_rates, w_gate, w_up, w_down):
    heads, dh, hid = w_gate.shape
    tokens = queries.shape[0]
    vmem = pl.BlockSpec(memory_space=pltpu.VMEM)
    hbm = pl.BlockSpec(memory_space=pltpu.HBM)
    tile = (dh // NZ, hid // NX)
    half = hid * heads // NX
    travel = jax.ShapeDtypeStruct((GROUPS, NX, PER, dh, hid // NX), BF16)
    out = jax.ShapeDtypeStruct((tokens, heads * dh), BF16)
    weights = jax.ShapeDtypeStruct((heads, dh, hid), BF16)
    given = (queries, keys, values, token_rates, w_gate, w_up, w_down)
    given = [pltpu.with_memory_space_constraint(a, pltpu.HBM) for a in given]
    applied, total = pl.pallas_call(
        main_kernel,
        name="grads_and_sum",
        out_shape=(out, travel),
        in_specs=[hbm] * 7,
        out_specs=(vmem, vmem),
        scratch_shapes=[
            pltpu.VMEM(queries.shape, BF16),
            pltpu.VMEM((2, heads, tokens, dh), BF16),
            pltpu.VMEM(values.shape, BF16),
            pltpu.VMEM(token_rates.shape, F32),
            pltpu.VMEM(w_gate.shape, BF16),
            pltpu.VMEM(w_up.shape, BF16),
            pltpu.VMEM(w_down.shape, BF16),
            pltpu.VMEM((dh, half), BF16),
            pltpu.VMEM((dh, half), BF16),
            pltpu.VMEM((half, dh), BF16),
            pltpu.VMEM((NX - 1, 2, tokens, dh), BF16),
            pltpu.VMEM((GROUPS, dh, half), F32),
            pltpu.VMEM((GROUPS, PER, dh, hid // NX), BF16),
            pltpu.VMEM((GROUPS, 16, PER) + tile, BF16),
            pltpu.VMEM((GROUPS, 13, PER) + tile, BF16),
            pltpu.VMEM((GROUPS, 2, PER) + tile, BF16),
            pltpu.VMEM((GROUPS, 16, PER) + tile, BF16),
            pltpu.SemaphoreType.DMA((9 + heads,)),
            pltpu.SemaphoreType.DMA((2 * KINDS, GROUPS)),
        ],
        compiler_params=pltpu.CompilerParams(
            collective_id=0, has_side_effects=True, vmem_limit_bytes=32 << 20
        ),
    )(*given)
    return pl.pallas_call(
        newton_kernel,
        name="newton",
        out_shape=(out, weights, weights, weights),
        in_specs=[vmem, vmem],
        out_specs=(hbm,) * 4,
        scratch_shapes=[
            pltpu.VMEM((heads * 3, dh, hid), BF16),
            pltpu.VMEM((heads * 3, dh, dh), BF16),
            pltpu.SemaphoreType.DMA((heads * 3 + 1,)),
        ],
        compiler_params=pltpu.CompilerParams(vmem_limit_bytes=24 << 20),
    )(total, applied)


def solution(mesh):
    in_specs = (
        P("seq", "head"),
        P("seq", "head"),
        P("seq", "head"),
        P("head", "seq"),
        P("head", None, None),
        P("head", None, None),
        P("head", None, None),
    )
    out_specs = (
        P("seq", "head"),
        P("head", None, None),
        P("head", None, None),
        P("head", None, None),
    )
    return jax.shard_map(
        per_device, mesh=mesh, in_specs=in_specs, out_specs=out_specs, check_vma=False
    )
```

```python
import math

import jax
import jax.numpy as jnp
from jax import lax
from jax.experimental import pallas as pl
from jax.experimental.pallas import tpu as pltpu
from jax.sharding import PartitionSpec as P

NS_STEPS = 5
NX = 4
NZ = 16
GROUPS = 3
PER = 2
F32 = jnp.float32
BF16 = jnp.bfloat16
MESH = pl.DeviceIdType.MESH


def dot(a, b, ca, cb):
    return lax.dot_general(a, b, (((ca,), (cb,)), ((), ())), preferred_element_type=F32)


def sigmoid(x):
    return 0.5 * jnp.tanh(0.5 * x) + 0.5


def wait_all(ref, sem):
    pltpu.make_async_copy(ref, ref, sem).wait()


def token_grads(k, vr, wg, wu, wd, s1, s2):
    gk = s1 * dot(k, wg, 1, 0)
    uk = s1 * dot(k, wu, 1, 0)
    dhid = -s2 * dot(vr, wd, 1, 1)
    sig = sigmoid(gk)
    silu = gk * sig
    hk = (silu * uk).astype(BF16)
    dg = (dhid * uk * (sig * (1.0 + gk * (1.0 - sig)))).astype(BF16)
    du = (dhid * silu).astype(BF16)
    kt = jnp.transpose(k)
    return (
        -s2 * dot(jnp.transpose(vr), hk, 1, 0),
        s1 * dot(kt, dg, 1, 0),
        s1 * dot(kt, du, 1, 0),
    )


def head_apply(h, q, wg, wu, wd):
    dh, hid = wg.shape[1:]
    s1, s2 = dh ** (-0.5), hid ** (-0.5)
    half = hid // 2
    total = None
    for j in range(2):
        js = slice(j * half, (j + 1) * half)
        gq = s1 * dot(q, wg[h, :, js], 1, 0)
        uq = s1 * dot(q, wu[h, :, js], 1, 0)
        hq = (gq * sigmoid(gq) * uq).astype(BF16)
        part = dot(hq, wd[h, js, :], 1, 0)
        total = part if total is None else total + part
    return (s2 * total).astype(BF16)


TOKENS, RELAY, NEAR, FAR, FILL, SIDE, PASS = range(7)
KINDS = 7
STRIDE = 5
STEPS = (1, 2, -1, -2)
LATENCY, INTERVAL = 3.0, 1.0


def main_kernel(
    q_hbm, k_hbm, v_hbm, r_hbm, wg_hbm, wu_hbm, wd_hbm, app_ref, o_ref,
    q_ref, k_ref, v_ref, r_ref, wg, wu, wd, wg_own, wu_own, wd_own, kv, acc, own,
    relay, near, got, far, spread, loads, sems,
):
    heads, dh, hid = wg.shape
    s1, s2 = dh ** (-0.5), hid ** (-0.5)
    me = lax.axis_index("seq")
    z, x = me // NX, me % NX
    right, left_x = (x + 1) % NX, (x + NX - 1) % NX
    split = NX // heads
    own_head, other_head = x % heads, (x + 1) % heads
    part = pl.ds(pl.multiple_of((x // heads) * (hid // split), hid // split), hid // split)

    def along_x(d):
        return z * NX + (x + d) % NX

    def along_z(d):
        return ((z + d) % NZ) * NX + x

    def send(src, dst, kind, group, peer):
        pltpu.make_async_remote_copy(
            src_ref=src,
            dst_ref=dst,
            send_sem=sems.at[kind, group],
            recv_sem=sems.at[KINDS + kind, group],
            device_id={"seq": peer},
            device_id_type=MESH,
        ).start()

    def arrived(ref, kind, group):
        wait_all(ref, sems.at[KINDS + kind, group])

    def left(ref, kind, group):
        wait_all(ref, sems.at[kind, group])

    def rows(d):
        return pl.ds(pl.multiple_of(((z + d) % NZ) * 16, 16), 16)

    copies = [(k_hbm.at[:, pl.ds(h * dh, dh)], k_ref.at[0, h]) for h in range(heads)]
    copies += [(r_hbm, r_ref), (v_hbm, v_ref)]
    copies += [
        (wg_hbm.at[own_head, :, part], wg_own),
        (wu_hbm.at[own_head, :, part], wu_own),
        (wd_hbm.at[own_head, part], wd_own),
        (q_hbm, q_ref),
        (wg_hbm, wg),
        (wu_hbm, wu),
        (wd_hbm, wd),
    ]
    copies = [pltpu.make_async_copy(a, b, loads.at[i]) for i, (a, b) in enumerate(copies)]
    for copy in copies:
        copy.start()
    barrier = pltpu.get_barrier_semaphore()
    peers = [along_x(d) for d in (1, -1)]
    peers += [along_z(d) for d in (1, -1, 2, -2, 3, -3, 5, -5, 6, -6)]
    for peer in peers:
        pl.semaphore_signal(barrier, inc=1, device_id={"seq": peer}, device_id_type=MESH)

    def start_z(g):
        def chunk(d):
            return own[g, :, rows(d)]

        for j, t in enumerate(STEPS):
            for i in range(3):
                near[g, 3 * j + i] = chunk(t + STRIDE * (i - 1))
            send(near.at[g, pl.ds(3 * j, 3)], got.at[g, pl.ds(3 * j, 3)], NEAR, g, along_z(t))
        near[g, 12] = chunk(-8)
        send(near.at[g, 12], got.at[g, 12], NEAR, g, along_z(-3))
        for i in range(3):
            near[g, 13 + i] = chunk(STRIDE * (i - 1))

    def collect(g):
        arrived(got.at[g], NEAR, g)
        for i in (0, 2, 1):
            total = near[g, 13 + i].astype(F32)
            for j in range(4):
                total = total + got[g, 3 * j + i].astype(F32)
            if i == 0:
                total = total + got[g, 12].astype(F32)
            near[g, 13 + i] = total.astype(BF16)
        send(near.at[g, pl.ds(14, 2)], far.at[g, pl.ds(0, 2)], FAR, g, along_z(STRIDE))
        send(near.at[g, pl.ds(13, 2)], far.at[g, pl.ds(2, 2)], FAR, g, along_z(-STRIDE))
        send(near.at[g, 13], far.at[g, 4], FAR, g, along_z(-2 * STRIDE))
        send(near.at[g, 15], far.at[g, 5], FAR, g, along_z(2 * STRIDE))

    def fill(g):
        arrived(far.at[g], FAR, g)
        parts = ((far[g, 5], far[g, 0], near[g, 13]), (far[g, 1], near[g, 14], far[g, 2]))
        parts += ((near[g, 15], far[g, 3], far[g, 4]),)
        for i, (a, b, c) in enumerate(parts):
            spread[g, i] = (a.astype(F32) + b.astype(F32) + c.astype(F32)).astype(BF16)
        for j, t in enumerate(STEPS):
            mine = spread.at[g, pl.ds(0, 3)]
            send(mine, spread.at[g, pl.ds(3 + 3 * j, 3)], FILL, g, along_z(t))
        send(spread.at[g, 0], spread.at[g, 15], FILL, g, along_z(3))

    def side(g):
        arrived(got.at[g], FILL, g)
        for j, t in enumerate((0,) + STEPS):
            for i in range(3):
                o_ref[g, x, :, rows(STRIDE * (i - 1) - t)] = spread[g, 3 * j + i]
        o_ref[g, x, :, rows(8)] = spread[g, 15]
        for d in (1, -1):
            send(o_ref.at[g, x], o_ref.at[g, x], SIDE, g, along_x(d))

    def pass_on(g):
        arrived(o_ref.at[g, pl.ds(0, 2)], SIDE, g)
        send(o_ref.at[g, left_x, 0], o_ref.at[g, left_x, 0], PASS, g, along_x(1))
        send(o_ref.at[g, right, 1], o_ref.at[g, right, 1], PASS, g, along_x(-1))

    def end(g):
        arrived(o_ref.at[g, 0], PASS, g)

    def send_tokens(i, relayed):
        send(k_ref.at[i, own_head], relay.at[i], RELAY, i, along_x(relayed))
        for d in (1, 3):
            send(k_ref.at[i, other_head], kv.at[d - 1, i], TOKENS, d - 1, along_x(d))

    for copy in copies[:heads]:
        copy.wait()
    pl.semaphore_wait(barrier, len(peers))
    send_tokens(0, 1)
    for copy in copies[heads : heads + 2]:
        copy.wait()
    rates = jnp.transpose(r_ref[...])
    for h in range(heads):
        v = v_ref[:, h * dh : (h + 1) * dh].astype(F32)
        k_ref[1, h] = (rates[:, h : h + 1] * v).astype(BF16)
    send_tokens(1, -1)
    for copy in copies[2 + heads : 5 + heads]:
        copy.wait()
    weights = (wg_own[...], wu_own[...], wd_own[...], s1, s2)
    for g, grad in enumerate(token_grads(k_ref[0, own_head], k_ref[1, own_head], *weights)):
        acc[g] = grad
    for i, d in ((0, 1), (1, -1)):
        arrived(relay.at[i], RELAY, i)
        send(relay.at[i], kv.at[1, i], TOKENS, 1, along_x(d))
    for copy in copies[5 + heads :]:
        copy.wait()
    for h in range(heads):
        cols = slice(h * dh, (h + 1) * dh)
        app_ref[:, cols] = head_apply(h, q_ref[:, cols], wg, wu, wd)
    for d in (1, 3):
        arrived(kv.at[d - 1], TOKENS, d - 1)
        for g, grad in enumerate(token_grads(kv[d - 1, 0], kv[d - 1, 1], *weights)):
            acc[g] = acc[g] + grad
    arrived(kv.at[1], TOKENS, 1)
    for g, grad in enumerate(token_grads(kv[1, 0], kv[1, 1], *weights)):
        total = (acc[g] + grad).astype(BF16)
        for c in range(PER):
            own[g, c] = total[:, c * 128 : (c + 1) * 128]
        start_z(g)
    stages = (collect, fill, side, pass_on, end)
    order = sorted(
        (LATENCY * s + INTERVAL * g, s, g) for s in range(len(stages)) for g in range(GROUPS)
    )
    for _, s, g in order:
        stages[s](g)
    for i in range(2):
        left(relay.at[i], RELAY, i)
    for g in range(GROUPS):
        left(kv.at[g], TOKENS, g)
        left(got.at[g], NEAR, g)
        left(far.at[g], FAR, g)
        left(got.at[g], FILL, g)
        left(o_ref.at[g, pl.ds(0, 2)], SIDE, g)
        left(o_ref.at[g, 0], PASS, g)


def newton_kernel(
    t_ref, applied_ref, applied_hbm, gate_hbm, up_hbm, down_hbm, x_ref, a_ref, sems
):
    outs = (gate_hbm, up_hbm, down_hbm)
    heads, _, hid = gate_hbm.shape
    handed = pltpu.make_async_copy(applied_ref, applied_hbm, sems.at[heads * 3])
    handed.start()
    where = [(h, kind) for h in range(heads) for kind in (2, 0, 1)]
    for m, (h, kind) in enumerate(where):
        blocks = [divmod(i, PER) for i in range(hid // 128)]
        total = jnp.concatenate(
            [t_ref[(kind + 1) % 3, heads * c + h, i].astype(F32) for c, i in blocks], axis=1
        )
        norm = jnp.sqrt(jnp.sum(total * total, keepdims=True)) + 1e-07
        x_ref[m] = (total / norm).astype(BF16)

    for s in range(NS_STEPS):
        for m in range(len(where)):
            x = x_ref[m]
            a_ref[m] = dot(x, x, 1, 1).astype(BF16)
        for m in range(len(where)):
            a = a_ref[m]
            b = -4.775 * a.astype(F32) + 2.0315 * dot(a, a, 1, 0)
            a_ref[m] = b.astype(BF16)
        for m in range(len(where)):
            x = x_ref[m]
            nxt = 3.4445 * x.astype(F32) + dot(a_ref[m], x, 1, 0)
            if s == NS_STEPS - 1:
                nxt = nxt * (0.2 * math.sqrt(hid))
            x_ref[m] = nxt.astype(BF16)
            if s == NS_STEPS - 1:
                h, kind = where[m]
                pltpu.make_async_copy(x_ref.at[m], outs[kind].at[h], sems.at[m]).start()
    for m, (h, kind) in enumerate(where):
        pltpu.make_async_copy(x_ref.at[m], outs[kind].at[h], sems.at[m]).wait()
    handed.wait()


def per_device(queries, keys, values, token_rates, w_gate, w_up, w_down):
    heads, dh, hid = w_gate.shape
    tokens = queries.shape[0]
    vmem = pl.BlockSpec(memory_space=pltpu.VMEM)
    hbm = pl.BlockSpec(memory_space=pltpu.HBM)
    tile = (dh // NZ, hid // NX)
    half = hid * heads // NX
    travel = jax.ShapeDtypeStruct((GROUPS, NX, PER, dh, hid // NX), BF16)
    out = jax.ShapeDtypeStruct((tokens, heads * dh), BF16)
    weights = jax.ShapeDtypeStruct((heads, dh, hid), BF16)
    given = (queries, keys, values, token_rates, w_gate, w_up, w_down)
    given = [pltpu.with_memory_space_constraint(a, pltpu.HBM) for a in given]
    applied, total = pl.pallas_call(
        main_kernel,
        name="grads_and_sum",
        out_shape=(out, travel),
        in_specs=[hbm] * 7,
        out_specs=(vmem, vmem),
        scratch_shapes=[
            pltpu.VMEM(queries.shape, BF16),
            pltpu.VMEM((2, heads, tokens, dh), BF16),
            pltpu.VMEM(values.shape, BF16),
            pltpu.VMEM(token_rates.shape, F32),
            pltpu.VMEM(w_gate.shape, BF16),
            pltpu.VMEM(w_up.shape, BF16),
            pltpu.VMEM(w_down.shape, BF16),
            pltpu.VMEM((dh, half), BF16),
            pltpu.VMEM((dh, half), BF16),
            pltpu.VMEM((half, dh), BF16),
            pltpu.VMEM((NX - 1, 2, tokens, dh), BF16),
            pltpu.VMEM((GROUPS, dh, half), F32),
            pltpu.VMEM((GROUPS, PER, dh, hid // NX), BF16),
            pltpu.VMEM((2, tokens, dh), BF16),
            pltpu.VMEM((GROUPS, 16, PER) + tile, BF16),
            pltpu.VMEM((GROUPS, 13, PER) + tile, BF16),
            pltpu.VMEM((GROUPS, 6, PER) + tile, BF16),
            pltpu.VMEM((GROUPS, 16, PER) + tile, BF16),
            pltpu.SemaphoreType.DMA((9 + heads,)),
            pltpu.SemaphoreType.DMA((2 * KINDS, GROUPS)),
        ],
        compiler_params=pltpu.CompilerParams(
            collective_id=0, has_side_effects=True, vmem_limit_bytes=32 << 20
        ),
    )(*given)
    return pl.pallas_call(
        newton_kernel,
        name="newton",
        out_shape=(out, weights, weights, weights),
        in_specs=[vmem, vmem],
        out_specs=(hbm,) * 4,
        scratch_shapes=[
            pltpu.VMEM((heads * 3, dh, hid), BF16),
            pltpu.VMEM((heads * 3, dh, dh), BF16),
            pltpu.SemaphoreType.DMA((heads * 3 + 1,)),
        ],
        compiler_params=pltpu.CompilerParams(vmem_limit_bytes=24 << 20),
    )(total, applied)


def solution(mesh):
    in_specs = (
        P("seq", "head"),
        P("seq", "head"),
        P("seq", "head"),
        P("head", "seq"),
        P("head", None, None),
        P("head", None, None),
        P("head", None, None),
    )
    out_specs = (
        P("seq", "head"),
        P("head", None, None),
        P("head", None, None),
        P("head", None, None),
    )
    return jax.shard_map(
        per_device, mesh=mesh, in_specs=in_specs, out_specs=out_specs, check_vma=False
    )
```

```python
import math

import jax
import jax.numpy as jnp
from jax import lax
from jax.experimental import pallas as pl
from jax.experimental.pallas import tpu as pltpu
from jax.sharding import PartitionSpec as P

NS_STEPS = 5
NX = 4
NZ = 16
GROUPS = 6
PER = 1
SLOTS = 6
F32 = jnp.float32
BF16 = jnp.bfloat16
MESH = pl.DeviceIdType.MESH


def dot(a, b, ca, cb):
    return lax.dot_general(a, b, (((ca,), (cb,)), ((), ())), preferred_element_type=F32)


def sigmoid(x):
    return 0.5 * jnp.tanh(0.5 * x) + 0.5


def wait_all(ref, sem):
    pltpu.make_async_copy(ref, ref, sem).wait()


def token_grads(k, vr, wg, wu, wd, s1, s2):
    gk = s1 * dot(k, wg, 1, 0)
    uk = s1 * dot(k, wu, 1, 0)
    dhid = -s2 * dot(vr, wd, 1, 1)
    sig = sigmoid(gk)
    silu = gk * sig
    hk = (silu * uk).astype(BF16)
    dg = (dhid * uk * (sig * (1.0 + gk * (1.0 - sig)))).astype(BF16)
    du = (dhid * silu).astype(BF16)
    kt = jnp.transpose(k)
    return (
        -s2 * dot(jnp.transpose(vr), hk, 1, 0),
        s1 * dot(kt, dg, 1, 0),
        s1 * dot(kt, du, 1, 0),
    )


def head_apply(h, q, wg, wu, wd):
    dh, hid = wg.shape[1:]
    s1, s2 = dh ** (-0.5), hid ** (-0.5)
    half = hid // 2
    total = None
    for j in range(2):
        js = slice(j * half, (j + 1) * half)
        gq = s1 * dot(q, wg[h, :, js], 1, 0)
        uq = s1 * dot(q, wu[h, :, js], 1, 0)
        hq = (gq * sigmoid(gq) * uq).astype(BF16)
        part = dot(hq, wd[h, js, :], 1, 0)
        total = part if total is None else total + part
    return (s2 * total).astype(BF16)


TOKENS, RATES, RELAY, NEAR, FAR, FILL, SIDE, PASS = range(8)
KINDS = 8
STRIDE = 5
STEPS = (1, 2, -1, -2)


def main_kernel(
    q_hbm, k_hbm, v_hbm, r_hbm, wg_hbm, wu_hbm, wd_hbm, app_ref, o_ref,
    q_ref, wg, wu, wd, wg_own, wu_own, wd_own, kv, rates, acc, own,
    relay, near, got, far, spread, loads, sems, beyond,
):
    heads, dh, hid = wg.shape
    s1, s2 = dh ** (-0.5), hid ** (-0.5)
    me = lax.axis_index("seq")
    z, x = me // NX, me % NX
    right, left_x = (x + 1) % NX, (x + NX - 1) % NX
    split = NX // heads
    own_head, other_head = x % heads, (x + 1) % heads
    part = pl.ds(pl.multiple_of((x // heads) * (hid // split), hid // split), hid // split)

    def along_x(d):
        return z * NX + (x + d) % NX

    def along_z(d):
        return ((z + d) % NZ) * NX + x

    def send(src, dst, kind, group, peer):
        pltpu.make_async_remote_copy(
            src_ref=src,
            dst_ref=dst,
            send_sem=sems.at[kind, group],
            recv_sem=sems.at[KINDS + kind, group],
            device_id={"seq": peer},
            device_id_type=MESH,
        ).start()

    def arrived(ref, kind, group):
        wait_all(ref, sems.at[KINDS + kind, group])

    def left(ref, kind, group):
        wait_all(ref, sems.at[kind, group])

    def rows(d):
        return pl.ds(pl.multiple_of(((z + d) % NZ) * 16, 16), 16)

    own_cols = pl.ds(pl.multiple_of(own_head * dh, dh), dh)
    other_cols = pl.ds(pl.multiple_of(other_head * dh, dh), dh)
    copies = [
        (k_hbm.at[:, own_cols], kv.at[0, 0]),
        (wg_hbm.at[own_head, :, part], wg_own),
        (wu_hbm.at[own_head, :, part], wu_own),
        (v_hbm.at[:, own_cols], kv.at[0, 1]),
        (r_hbm, rates.at[0]),
        (wd_hbm.at[own_head, part], wd_own),
        (q_hbm, q_ref),
        (wg_hbm, wg),
        (wu_hbm, wu),
        (wd_hbm, wd),
    ]
    barrier = pltpu.get_barrier_semaphore()
    peers = [along_x(d) for d in (1, -1)]
    peers += [along_z(d) for d in (1, -1, 2, -2, 3, -3)]
    for peer in peers:
        pl.semaphore_signal(barrier, inc=1, device_id={"seq": peer}, device_id_type=MESH)
    copies = [pltpu.make_async_copy(a, b, loads.at[i]) for i, (a, b) in enumerate(copies)]
    for copy in copies:
        copy.start()

    def start_z(g):
        def chunk(d):
            return own[g, :, rows(d)]

        for j, t in enumerate(STEPS):
            for i in range(3):
                near[g, 3 * j + i] = chunk(t + STRIDE * (i - 1))
            send(near.at[g, pl.ds(3 * j, 3)], got.at[g, pl.ds(3 * j, 3)], NEAR, g, along_z(t))
        near[g, 12] = chunk(-8)
        send(near.at[g, 12], got.at[g, 12], NEAR, g, along_z(-3))
        for i in range(3):
            near[g, 13 + i] = chunk(STRIDE * (i - 1))

    def collect(g):
        arrived(got.at[g], NEAR, g)
        for i in (0, 2, 1):
            total = near[g, 13 + i].astype(F32)
            for j in range(4):
                total = total + got[g, 3 * j + i].astype(F32)
            if i == 0:
                total = total + got[g, 12].astype(F32)
            near[g, 13 + i] = total.astype(BF16)
        send(near.at[g, pl.ds(14, 2)], far.at[g, pl.ds(0, 2)], FAR, g, along_z(STRIDE))
        send(near.at[g, pl.ds(13, 2)], far.at[g, pl.ds(2, 2)], FAR, g, along_z(-STRIDE))
        send(near.at[g, 13], far.at[g, 4], FAR, g, along_z(-2 * STRIDE))
        send(near.at[g, 15], far.at[g, 5], FAR, g, along_z(2 * STRIDE))

    def fill(g):
        arrived(far.at[g], FAR, g)
        parts = ((far[g, 5], far[g, 0], near[g, 13]), (far[g, 1], near[g, 14], far[g, 2]))
        parts += ((near[g, 15], far[g, 3], far[g, 4]),)
        for i, (a, b, c) in enumerate(parts):
            spread[g, i] = (a.astype(F32) + b.astype(F32) + c.astype(F32)).astype(BF16)
        for j, t in enumerate(STEPS):
            mine = spread.at[g, pl.ds(0, 3)]
            send(mine, spread.at[g, pl.ds(3 + 3 * j, 3)], FILL, g, along_z(t))
        send(spread.at[g, 0], spread.at[g, 15], FILL, g, along_z(3))

    def side(g):
        arrived(got.at[g], FILL, g)
        for j, t in enumerate((0,) + STEPS):
            for i in range(3):
                o_ref[g, x, :, rows(STRIDE * (i - 1) - t)] = spread[g, 3 * j + i]
        o_ref[g, x, :, rows(8)] = spread[g, 15]
        for d in (1, -1):
            send(o_ref.at[g, x], o_ref.at[g, x], SIDE, g, along_x(d))

    def pass_on(g):
        arrived(o_ref.at[g, pl.ds(0, 2)], SIDE, g)
        for origin, at, d in ((left_x, 0, 1), (right, dh // 2, -1)):
            piece = o_ref.at[g, origin, :, pl.ds(at, dh // 2)]
            send(piece, piece, PASS, g, along_x(d))

    def end(g):
        arrived(o_ref.at[g, 0], PASS, g)

    pl.semaphore_wait(barrier, len(peers))
    for d in (3, -3):
        pl.semaphore_signal(
            beyond, inc=1, device_id={"seq": along_z(d)}, device_id_type=MESH
        )
    for i, (array, d) in enumerate(((k_hbm, 1), (v_hbm, -1))):
        send(array.at[:, own_cols], relay.at[i], RELAY, i, along_x(d))
    send(r_hbm, rates.at[1], RATES, 1, along_x(1))
    send(r_hbm, rates.at[3], RATES, 3, along_x(-1))
    for i, array in enumerate((k_hbm, v_hbm)):
        for d in (1, 3):
            send(array.at[:, other_cols], kv.at[d, i], TOKENS, d, along_x(d))
    for copy in copies[:6]:
        copy.wait()
    weights = (wg_own[...], wu_own[...], wd_own[...], s1, s2)

    def grads_from(d):
        rate = jnp.transpose(rates[d])
        rate = jnp.where(own_head == 0, rate[:, 0:1], rate[:, 1:2])
        vr = (rate * kv[d, 1].astype(F32)).astype(BF16)
        return enumerate(token_grads(kv[d, 0], vr, *weights))

    for i, grad in grads_from(0):
        acc[i] = grad
    for copy in copies[6:]:
        copy.wait()
    for h in range(heads):
        cols = slice(h * dh, (h + 1) * dh)
        app_ref[:, cols] = head_apply(h, q_ref[:, cols], wg, wu, wd)
    arrived(rates.at[1], RATES, 1)
    send(rates.at[1], rates.at[2], RATES, 2, along_x(1))
    for i, d in ((0, 1), (1, -1)):
        arrived(relay.at[i], RELAY, i)
        send(relay.at[i], kv.at[2, i], TOKENS, 2, along_x(d))
    arrived(rates.at[3], RATES, 3)
    for d in (1, 3):
        arrived(kv.at[d], TOKENS, d)
        for i, grad in grads_from(d):
            acc[i] = acc[i] + grad
    arrived(rates.at[2], RATES, 2)
    arrived(kv.at[2], TOKENS, 2)
    for i, grad in grads_from(2):
        total = (acc[i] + grad).astype(BF16)
        for c in range(2):
            own[divmod(2 * i + c, PER)] = total[:, c * 128 : (c + 1) * 128]
            if (2 * i + c + 1) % PER == 0:
                start_z((2 * i + c) // PER)
    pl.semaphore_wait(beyond, 2)
    stages = (collect, fill, side, pass_on, end)
    for stage in stages:
        for g in range(GROUPS):
            stage(g)
    for i in range(2):
        left(relay.at[i], RELAY, i)
    for d in range(1, NX):
        left(kv.at[d], TOKENS, d)
        left(rates.at[d], RATES, d)
    for g in range(GROUPS):
        left(got.at[g], NEAR, g)
        left(far.at[g], FAR, g)
        left(got.at[g], FILL, g)
        left(o_ref.at[g, pl.ds(0, 2)], SIDE, g)
        left(o_ref.at[g, 0], PASS, g)


def newton_kernel(
    t_ref, applied_ref, applied_hbm, gate_hbm, up_hbm, down_hbm, x_ref, a_ref, sems
):
    outs = (gate_hbm, up_hbm, down_hbm)
    heads, _, hid = gate_hbm.shape
    handed = pltpu.make_async_copy(applied_ref, applied_hbm, sems.at[heads * 3])
    handed.start()
    where = [(h, kind) for h in range(heads) for kind in (2, 0, 1)]
    norms = []
    for m, (h, kind) in enumerate(where):
        blocks = []
        for c in range(hid // 128):
            group, place = divmod(2 * ((kind + 1) % 3) + c % 2, PER)
            blocks.append(t_ref[group, heads * (c // 2) + h, place].astype(F32))
        total = jnp.concatenate(blocks, axis=1)
        norms.append(jnp.sqrt(jnp.sum(total * total, keepdims=True)) + 1e-07)
        x_ref[m] = total.astype(BF16)
    for s in range(NS_STEPS):
        for m in range(len(where)):
            x = x_ref[m]
            square = dot(x, x, 1, 1)
            if s == 0:
                square = square * (1.0 / norms[m]) * (1.0 / norms[m])
            a_ref[m] = square.astype(BF16)
        for m in range(len(where)):
            a = a_ref[m]
            b = -4.775 * a.astype(F32) + 2.0315 * dot(a, a, 1, 0)
            a_ref[m] = b.astype(BF16)
        for m in range(len(where)):
            x = x_ref[m]
            nxt = 3.4445 * x.astype(F32) + dot(a_ref[m], x, 1, 0)
            if s == 0:
                nxt = nxt * (1.0 / norms[m])
            if s == NS_STEPS - 1:
                nxt = nxt * (0.2 * math.sqrt(hid))
            x_ref[m] = nxt.astype(BF16)
            if s == NS_STEPS - 1:
                h, kind = where[m]
                pltpu.make_async_copy(x_ref.at[m], outs[kind].at[h], sems.at[m]).start()
    for m, (h, kind) in enumerate(where):
        pltpu.make_async_copy(x_ref.at[m], outs[kind].at[h], sems.at[m]).wait()
    handed.wait()


def per_device(queries, keys, values, token_rates, w_gate, w_up, w_down):
    heads, dh, hid = w_gate.shape
    tokens = queries.shape[0]
    vmem = pl.BlockSpec(memory_space=pltpu.VMEM)
    hbm = pl.BlockSpec(memory_space=pltpu.HBM)
    tile = (dh // NZ, hid // NX)
    half = hid * heads // NX
    travel = jax.ShapeDtypeStruct((GROUPS, NX, PER, dh, hid // NX), BF16)
    out = jax.ShapeDtypeStruct((tokens, heads * dh), BF16)
    weights = jax.ShapeDtypeStruct((heads, dh, hid), BF16)
    given = (queries, keys, values, token_rates, w_gate, w_up, w_down)
    given = [pltpu.with_memory_space_constraint(a, pltpu.HBM) for a in given]
    applied, total = pl.pallas_call(
        main_kernel,
        name="grads_and_sum",
        out_shape=(out, travel),
        in_specs=[hbm] * 7,
        out_specs=(vmem, vmem),
        scratch_shapes=[
            pltpu.VMEM(queries.shape, BF16),
            pltpu.VMEM(w_gate.shape, BF16),
            pltpu.VMEM(w_up.shape, BF16),
            pltpu.VMEM(w_down.shape, BF16),
            pltpu.VMEM((dh, half), BF16),
            pltpu.VMEM((dh, half), BF16),
            pltpu.VMEM((half, dh), BF16),
            pltpu.VMEM((NX, 2, tokens, dh), BF16),
            pltpu.VMEM((NX,) + token_rates.shape, F32),
            pltpu.VMEM((3, dh, half), F32),
            pltpu.VMEM((GROUPS, PER, dh, hid // NX), BF16),
            pltpu.VMEM((2, tokens, dh), BF16),
            pltpu.VMEM((GROUPS, 16, PER) + tile, BF16),
            pltpu.VMEM((GROUPS, 13, PER) + tile, BF16),
            pltpu.VMEM((GROUPS, 6, PER) + tile, BF16),
            pltpu.VMEM((GROUPS, 16, PER) + tile, BF16),
            pltpu.SemaphoreType.DMA((10,)),
            pltpu.SemaphoreType.DMA((2 * KINDS, SLOTS)),
            pltpu.SemaphoreType.REGULAR,
        ],
        compiler_params=pltpu.CompilerParams(
            collective_id=0, has_side_effects=True, vmem_limit_bytes=32 << 20
        ),
    )(*given)
    return pl.pallas_call(
        newton_kernel,
        name="newton",
        out_shape=(out, weights, weights, weights),
        in_specs=[vmem, vmem],
        out_specs=(hbm,) * 4,
        scratch_shapes=[
            pltpu.VMEM((heads * 3, dh, hid), BF16),
            pltpu.VMEM((heads * 3, dh, dh), BF16),
            pltpu.SemaphoreType.DMA((heads * 3 + 1,)),
        ],
        compiler_params=pltpu.CompilerParams(vmem_limit_bytes=24 << 20),
    )(total, applied)


def solution(mesh):
    in_specs = (
        P("seq", "head"),
        P("seq", "head"),
        P("seq", "head"),
        P("head", "seq"),
        P("head", None, None),
        P("head", None, None),
        P("head", None, None),
    )
    out_specs = (
        P("seq", "head"),
        P("head", None, None),
        P("head", None, None),
        P("head", None, None),
    )
    return jax.shard_map(
        per_device, mesh=mesh, in_specs=in_specs, out_specs=out_specs, check_vma=False
    )
```

```python
import math

import jax
import jax.numpy as jnp
from jax import lax
from jax.experimental import pallas as pl
from jax.experimental.pallas import tpu as pltpu
from jax.sharding import PartitionSpec as P

NS_STEPS = 5
HEAD_START = 2
ORDER = (2, 0, 1)
NX = 4
NZ = 16
GROUPS = 6
PER = 1
SLOTS = 6
F32 = jnp.float32
BF16 = jnp.bfloat16
MESH = pl.DeviceIdType.MESH


def dot(a, b, ca, cb):
    return lax.dot_general(a, b, (((ca,), (cb,)), ((), ())), preferred_element_type=F32)


def sigmoid(x):
    return 0.5 * jnp.tanh(0.5 * x) + 0.5


def wait_all(ref, sem):
    pltpu.make_async_copy(ref, ref, sem).wait()


def token_grads(k, vr, wg, wu, wd, s1, s2):
    gk = s1 * dot(k, wg, 1, 0)
    uk = s1 * dot(k, wu, 1, 0)
    dhid = -s2 * dot(vr, wd, 1, 1)
    sig = sigmoid(gk)
    silu = gk * sig
    hk = (silu * uk).astype(BF16)
    dg = (dhid * uk * (sig * (1.0 + gk * (1.0 - sig)))).astype(BF16)
    du = (dhid * silu).astype(BF16)
    kt = jnp.transpose(k)
    return (
        -s2 * dot(jnp.transpose(vr), hk, 1, 0),
        s1 * dot(kt, dg, 1, 0),
        s1 * dot(kt, du, 1, 0),
    )


def head_apply(h, q, wg, wu, wd):
    dh, hid = wg.shape[1:]
    s1, s2 = dh ** (-0.5), hid ** (-0.5)
    half = hid // 2
    total = None
    for j in range(2):
        js = slice(j * half, (j + 1) * half)
        gq = s1 * dot(q, wg[h, :, js], 1, 0)
        uq = s1 * dot(q, wu[h, :, js], 1, 0)
        hq = (gq * sigmoid(gq) * uq).astype(BF16)
        part = dot(hq, wd[h, js, :], 1, 0)
        total = part if total is None else total + part
    return (s2 * total).astype(BF16)


TOKENS, RATES, RELAY, NEAR, FAR, FILL, SIDE, PASS = range(8)
KINDS = 8
STRIDE = 5
STEPS = (1, 2, -1, -2)


def main_kernel(
    q_hbm, k_hbm, v_hbm, r_hbm, wg_hbm, wu_hbm, wd_hbm, app_ref, o_ref, begun_ref,
    q_ref, wg, wu, wd, wg_own, wu_own, wd_own, kv, rates, acc, own,
    relay, near, got, far, spread, a_ref, loads, sems, beyond,
):
    heads, dh, hid = wg.shape
    s1, s2 = dh ** (-0.5), hid ** (-0.5)
    me = lax.axis_index("seq")
    z, x = me // NX, me % NX
    right, left_x = (x + 1) % NX, (x + NX - 1) % NX
    split = NX // heads
    own_head, other_head = x % heads, (x + 1) % heads
    part = pl.ds(pl.multiple_of((x // heads) * (hid // split), hid // split), hid // split)

    def along_x(d):
        return z * NX + (x + d) % NX

    def along_z(d):
        return ((z + d) % NZ) * NX + x

    def send(src, dst, kind, group, peer):
        pltpu.make_async_remote_copy(
            src_ref=src,
            dst_ref=dst,
            send_sem=sems.at[kind, group],
            recv_sem=sems.at[KINDS + kind, group],
            device_id={"seq": peer},
            device_id_type=MESH,
        ).start()

    def arrived(ref, kind, group):
        wait_all(ref, sems.at[KINDS + kind, group])

    def left(ref, kind, group):
        wait_all(ref, sems.at[kind, group])

    def rows(d):
        return pl.ds(pl.multiple_of(((z + d) % NZ) * 16, 16), 16)

    own_cols = pl.ds(pl.multiple_of(own_head * dh, dh), dh)
    other_cols = pl.ds(pl.multiple_of(other_head * dh, dh), dh)
    copies = [
        (k_hbm.at[:, own_cols], kv.at[0, 0]),
        (wg_hbm.at[own_head, :, part], wg_own),
        (wu_hbm.at[own_head, :, part], wu_own),
        (v_hbm.at[:, own_cols], kv.at[0, 1]),
        (r_hbm, rates.at[0]),
        (wd_hbm.at[own_head, part], wd_own),
        (q_hbm, q_ref),
        (wg_hbm, wg),
        (wu_hbm, wu),
        (wd_hbm, wd),
    ]
    barrier = pltpu.get_barrier_semaphore()
    peers = [along_x(d) for d in (1, -1)]
    peers += [along_z(d) for d in (1, -1, 2, -2, 3, -3)]
    for peer in peers:
        pl.semaphore_signal(barrier, inc=1, device_id={"seq": peer}, device_id_type=MESH)
    copies = [pltpu.make_async_copy(a, b, loads.at[i]) for i, (a, b) in enumerate(copies)]
    for copy in copies:
        copy.start()

    def start_z(g):
        def chunk(d):
            return own[g, :, rows(d)]

        for j, t in enumerate(STEPS):
            for i in range(3):
                near[g, 3 * j + i] = chunk(t + STRIDE * (i - 1))
            send(near.at[g, pl.ds(3 * j, 3)], got.at[g, pl.ds(3 * j, 3)], NEAR, g, along_z(t))
        near[g, 12] = chunk(-8)
        send(near.at[g, 12], got.at[g, 12], NEAR, g, along_z(-3))
        for i in range(3):
            near[g, 13 + i] = chunk(STRIDE * (i - 1))

    def collect(g):
        arrived(got.at[g], NEAR, g)
        for i in (0, 2, 1):
            total = near[g, 13 + i].astype(F32)
            for j in range(4):
                total = total + got[g, 3 * j + i].astype(F32)
            if i == 0:
                total = total + got[g, 12].astype(F32)
            near[g, 13 + i] = total.astype(BF16)
        send(near.at[g, pl.ds(14, 2)], far.at[g, pl.ds(0, 2)], FAR, g, along_z(STRIDE))
        send(near.at[g, pl.ds(13, 2)], far.at[g, pl.ds(2, 2)], FAR, g, along_z(-STRIDE))
        send(near.at[g, 13], far.at[g, 4], FAR, g, along_z(-2 * STRIDE))
        send(near.at[g, 15], far.at[g, 5], FAR, g, along_z(2 * STRIDE))

    def fill(g):
        arrived(far.at[g], FAR, g)
        parts = ((far[g, 5], far[g, 0], near[g, 13]), (far[g, 1], near[g, 14], far[g, 2]))
        parts += ((near[g, 15], far[g, 3], far[g, 4]),)
        for i, (a, b, c) in enumerate(parts):
            spread[g, i] = (a.astype(F32) + b.astype(F32) + c.astype(F32)).astype(BF16)
        for j, t in enumerate(STEPS):
            mine = spread.at[g, pl.ds(0, 3)]
            send(mine, spread.at[g, pl.ds(3 + 3 * j, 3)], FILL, g, along_z(t))
        send(spread.at[g, 0], spread.at[g, 15], FILL, g, along_z(3))

    def side(g):
        arrived(got.at[g], FILL, g)
        for j, t in enumerate((0,) + STEPS):
            for i in range(3):
                o_ref[g, x, :, rows(STRIDE * (i - 1) - t)] = spread[g, 3 * j + i]
        o_ref[g, x, :, rows(8)] = spread[g, 15]
        for d in (1, -1):
            send(o_ref.at[g, x], o_ref.at[g, x], SIDE, g, along_x(d))

    def pass_on(g):
        arrived(o_ref.at[g, pl.ds(0, 2)], SIDE, g)
        for origin, at, d in ((left_x, 0, 1), (right, dh // 2, -1)):
            piece = o_ref.at[g, origin, :, pl.ds(at, dh // 2)]
            send(piece, piece, PASS, g, along_x(d))

    def end(g):
        arrived(o_ref.at[g, 0], PASS, g)

    pl.semaphore_wait(barrier, len(peers))
    for d in (3, -3):
        pl.semaphore_signal(
            beyond, inc=1, device_id={"seq": along_z(d)}, device_id_type=MESH
        )
    for i, (array, d) in enumerate(((k_hbm, 1), (v_hbm, -1))):
        send(array.at[:, own_cols], relay.at[i], RELAY, i, along_x(d))
    send(r_hbm, rates.at[1], RATES, 1, along_x(1))
    send(r_hbm, rates.at[3], RATES, 3, along_x(-1))
    for i, array in enumerate((k_hbm, v_hbm)):
        for d in (1, 3):
            send(array.at[:, other_cols], kv.at[d, i], TOKENS, d, along_x(d))
    for copy in copies[:6]:
        copy.wait()
    weights = (wg_own[...], wu_own[...], wd_own[...], s1, s2)

    def grads_from(d):
        rate = jnp.transpose(rates[d])
        rate = jnp.where(own_head == 0, rate[:, 0:1], rate[:, 1:2])
        vr = (rate * kv[d, 1].astype(F32)).astype(BF16)
        return enumerate(token_grads(kv[d, 0], vr, *weights))

    for i, grad in grads_from(0):
        acc[i] = grad
    for copy in copies[6:]:
        copy.wait()
    for h in range(heads):
        cols = slice(h * dh, (h + 1) * dh)
        app_ref[:, cols] = head_apply(h, q_ref[:, cols], wg, wu, wd)
    arrived(rates.at[1], RATES, 1)
    send(rates.at[1], rates.at[2], RATES, 2, along_x(1))
    for i, d in ((0, 1), (1, -1)):
        arrived(relay.at[i], RELAY, i)
        send(relay.at[i], kv.at[2, i], TOKENS, 2, along_x(d))
    arrived(rates.at[3], RATES, 3)
    for d in (1, 3):
        arrived(kv.at[d], TOKENS, d)
        for i, grad in grads_from(d):
            acc[i] = acc[i] + grad
    arrived(rates.at[2], RATES, 2)
    arrived(kv.at[2], TOKENS, 2)
    for i, grad in grads_from(2):
        total = (acc[i] + grad).astype(BF16)
        for c in range(2):
            own[divmod(2 * i + c, PER)] = total[:, c * 128 : (c + 1) * 128]
            if (2 * i + c + 1) % PER == 0:
                start_z((2 * i + c) // PER)
    pl.semaphore_wait(beyond, 2)
    stages = (collect, fill, side, pass_on)
    for stage in stages:
        for g in range(GROUPS):
            stage(g)
    early = begun_ref.shape[0]
    ready = GROUPS * early // (3 * heads)
    for g in range(ready):
        end(g)
    where = [(h, kind) for kind in ORDER for h in range(heads)]
    scales = [newton_start(o_ref, begun_ref, m, *where[m], heads) for m in range(early)]
    for s in range(HEAD_START):
        for _ in newton_step(begun_ref, a_ref, range(early), s, scales):
            pass
    for g in range(ready, GROUPS):
        end(g)
    for i in range(2):
        left(relay.at[i], RELAY, i)
    for d in range(1, NX):
        left(kv.at[d], TOKENS, d)
        left(rates.at[d], RATES, d)
    for g in range(GROUPS):
        left(got.at[g], NEAR, g)
        left(far.at[g], FAR, g)
        left(got.at[g], FILL, g)
        left(o_ref.at[g, pl.ds(0, 2)], SIDE, g)
        left(o_ref.at[g, 0], PASS, g)


def newton_start(t_ref, x_ref, m, h, kind, heads):
    blocks = []
    for c in range(NX):
        group, place = divmod(2 * ((kind + 1) % 3) + c % 2, PER)
        blocks.append(t_ref[group, heads * (c // 2) + h, place].astype(F32))
    total = jnp.concatenate(blocks, axis=1)
    x_ref[m] = total.astype(BF16)
    return 1.0 / (jnp.sqrt(jnp.sum(total * total, keepdims=True)) + 1e-07)


def newton_step(x_ref, a_ref, mats, s, scales):
    for m in mats:
        x = x_ref[m]
        square = dot(x, x, 1, 1)
        if s == 0:
            square = square * scales[m] * scales[m]
        a_ref[m] = square.astype(BF16)
    for m in mats:
        a = a_ref[m]
        a_ref[m] = (-4.775 * a.astype(F32) + 2.0315 * dot(a, a, 1, 0)).astype(BF16)
    for m in mats:
        x = x_ref[m]
        nxt = 3.4445 * x.astype(F32) + dot(a_ref[m], x, 1, 0)
        if s == 0:
            nxt = nxt * scales[m]
        if s == NS_STEPS - 1:
            nxt = nxt * (0.2 * math.sqrt(x.shape[1]))
        x_ref[m] = nxt.astype(BF16)
        yield m


def newton_kernel(
    t_ref, begun_ref, applied_ref, applied_hbm, gate_hbm, up_hbm, down_hbm, x_ref, a_ref, sems
):
    outs = (gate_hbm, up_hbm, down_hbm)
    heads = gate_hbm.shape[0]
    handed = pltpu.make_async_copy(applied_ref, applied_hbm, sems.at[heads * 3])
    handed.start()
    where = [(h, kind) for kind in ORDER for h in range(heads)]
    early = begun_ref.shape[0]
    scales = {}
    for m in range(early, len(where)):
        scales[m] = newton_start(t_ref, x_ref, m, *where[m], heads)
    for s in range(NS_STEPS):
        mats = range(early, len(where))
        if s >= HEAD_START:
            mats = range(len(where))
        if s == HEAD_START:
            x_ref[pl.ds(0, early)] = begun_ref[...]
        for m in newton_step(x_ref, a_ref, mats, s, scales):
            if s == NS_STEPS - 1:
                h, kind = where[m]
                pltpu.make_async_copy(x_ref.at[m], outs[kind].at[h], sems.at[m]).start()
    for m, (h, kind) in enumerate(where):
        pltpu.make_async_copy(x_ref.at[m], outs[kind].at[h], sems.at[m]).wait()
    handed.wait()


def per_device(queries, keys, values, token_rates, w_gate, w_up, w_down):
    heads, dh, hid = w_gate.shape
    tokens = queries.shape[0]
    vmem = pl.BlockSpec(memory_space=pltpu.VMEM)
    hbm = pl.BlockSpec(memory_space=pltpu.HBM)
    tile = (dh // NZ, hid // NX)
    half = hid * heads // NX
    travel = jax.ShapeDtypeStruct((GROUPS, NX, PER, dh, hid // NX), BF16)
    out = jax.ShapeDtypeStruct((tokens, heads * dh), BF16)
    weights = jax.ShapeDtypeStruct((heads, dh, hid), BF16)
    given = (queries, keys, values, token_rates, w_gate, w_up, w_down)
    given = [pltpu.with_memory_space_constraint(a, pltpu.HBM) for a in given]
    begun = jax.ShapeDtypeStruct((heads * 2, dh, hid), BF16)
    applied, total, begun = pl.pallas_call(
        main_kernel,
        name="grads_and_sum",
        out_shape=(out, travel, begun),
        in_specs=[hbm] * 7,
        out_specs=(vmem,) * 3,
        scratch_shapes=[
            pltpu.VMEM(queries.shape, BF16),
            pltpu.VMEM(w_gate.shape, BF16),
            pltpu.VMEM(w_up.shape, BF16),
            pltpu.VMEM(w_down.shape, BF16),
            pltpu.VMEM((dh, half), BF16),
            pltpu.VMEM((dh, half), BF16),
            pltpu.VMEM((half, dh), BF16),
            pltpu.VMEM((NX, 2, tokens, dh), BF16),
            pltpu.VMEM((NX,) + token_rates.shape, F32),
            pltpu.VMEM((3, dh, half), F32),
            pltpu.VMEM((GROUPS, PER, dh, hid // NX), BF16),
            pltpu.VMEM((2, tokens, dh), BF16),
            pltpu.VMEM((GROUPS, 16, PER) + tile, BF16),
            pltpu.VMEM((GROUPS, 13, PER) + tile, BF16),
            pltpu.VMEM((GROUPS, 6, PER) + tile, BF16),
            pltpu.VMEM((GROUPS, 16, PER) + tile, BF16),
            pltpu.VMEM((heads * 2, dh, dh), BF16),
            pltpu.SemaphoreType.DMA((10,)),
            pltpu.SemaphoreType.DMA((2 * KINDS, SLOTS)),
            pltpu.SemaphoreType.REGULAR,
        ],
        compiler_params=pltpu.CompilerParams(
            collective_id=0, has_side_effects=True, vmem_limit_bytes=32 << 20
        ),
    )(*given)
    return pl.pallas_call(
        newton_kernel,
        name="newton",
        out_shape=(out, weights, weights, weights),
        in_specs=[vmem] * 3,
        out_specs=(hbm,) * 4,
        scratch_shapes=[
            pltpu.VMEM((heads * 3, dh, hid), BF16),
            pltpu.VMEM((heads * 3, dh, dh), BF16),
            pltpu.SemaphoreType.DMA((heads * 3 + 1,)),
        ],
        compiler_params=pltpu.CompilerParams(vmem_limit_bytes=24 << 20),
    )(total, begun, applied)


def solution(mesh):
    in_specs = (
        P("seq", "head"),
        P("seq", "head"),
        P("seq", "head"),
        P("head", "seq"),
        P("head", None, None),
        P("head", None, None),
        P("head", None, None),
    )
    out_specs = (
        P("seq", "head"),
        P("head", None, None),
        P("head", None, None),
        P("head", None, None),
    )
    return jax.shard_map(
        per_device, mesh=mesh, in_specs=in_specs, out_specs=out_specs, check_vma=False
    )
```

```python
import math

import jax
import jax.numpy as jnp
from jax import lax
from jax.experimental import pallas as pl
from jax.experimental.pallas import tpu as pltpu
from jax.sharding import PartitionSpec as P

NS_STEPS = 5
HEAD_START = 2
ORDER = (2, 0, 1)
NX = 4
NZ = 16
GROUPS = 6
PER = 1
SLOTS = 6
F32 = jnp.float32
BF16 = jnp.bfloat16
MESH = pl.DeviceIdType.MESH


def dot(a, b, ca, cb):
    return lax.dot_general(a, b, (((ca,), (cb,)), ((), ())), preferred_element_type=F32)


def sigmoid(x):
    return 0.5 * jnp.tanh(0.5 * x) + 0.5


def wait_all(ref, sem):
    pltpu.make_async_copy(ref, ref, sem).wait()


def token_grads(k, vr, wg, wu, wd, s1, s2):
    gk = s1 * dot(k, wg, 1, 0)
    uk = s1 * dot(k, wu, 1, 0)
    dhid = -s2 * dot(vr, wd, 1, 1)
    sig = sigmoid(gk)
    silu = gk * sig
    hk = (silu * uk).astype(BF16)
    dg = (dhid * uk * (sig * (1.0 + gk * (1.0 - sig)))).astype(BF16)
    du = (dhid * silu).astype(BF16)
    kt = jnp.transpose(k)
    return (
        -s2 * dot(jnp.transpose(vr), hk, 1, 0),
        s1 * dot(kt, dg, 1, 0),
        s1 * dot(kt, du, 1, 0),
    )


def head_apply(h, q, wg, wu, wd):
    dh, hid = wg.shape[1:]
    s1, s2 = dh ** (-0.5), hid ** (-0.5)
    half = hid // 2
    total = None
    for j in range(2):
        js = slice(j * half, (j + 1) * half)
        gq = s1 * dot(q, wg[h, :, js], 1, 0)
        uq = s1 * dot(q, wu[h, :, js], 1, 0)
        hq = (gq * sigmoid(gq) * uq).astype(BF16)
        part = dot(hq, wd[h, js, :], 1, 0)
        total = part if total is None else total + part
    return (s2 * total).astype(BF16)


TOKENS, RATES, RELAY, NEAR, FAR, FILL, SIDE, PASS = range(8)
KINDS = 8
STRIDE = 5
STEPS = (1, 2, -1, -2)


def main_kernel(
    q_hbm, k_hbm, v_hbm, r_hbm, wg_hbm, wu_hbm, wd_hbm, app_ref, o_ref, begun_ref,
    q_ref, wg, wu, wd, wg_own, wu_own, wd_own, kv, rates, acc, own,
    relay, near, got, far, spread, a_ref, loads, sems, beyond,
):
    heads, dh, hid = wg.shape
    s1, s2 = dh ** (-0.5), hid ** (-0.5)
    me = lax.axis_index("seq")
    z, x = me // NX, me % NX
    right, left_x = (x + 1) % NX, (x + NX - 1) % NX
    split = NX // heads
    own_head, other_head = x % heads, (x + 1) % heads
    part = pl.ds(pl.multiple_of((x // heads) * (hid // split), hid // split), hid // split)

    def along_x(d):
        return z * NX + (x + d) % NX

    def along_z(d):
        return ((z + d) % NZ) * NX + x

    def send(src, dst, kind, group, peer):
        pltpu.make_async_remote_copy(
            src_ref=src,
            dst_ref=dst,
            send_sem=sems.at[kind, group],
            recv_sem=sems.at[KINDS + kind, group],
            device_id={"seq": peer},
            device_id_type=MESH,
        ).start()

    def arrived(ref, kind, group):
        wait_all(ref, sems.at[KINDS + kind, group])

    def left(ref, kind, group):
        wait_all(ref, sems.at[kind, group])

    def rows(d):
        return pl.ds(pl.multiple_of(((z + d) % NZ) * 16, 16), 16)

    own_cols = pl.ds(pl.multiple_of(own_head * dh, dh), dh)
    other_cols = pl.ds(pl.multiple_of(other_head * dh, dh), dh)
    copies = [
        (k_hbm.at[:, own_cols], kv.at[0, 0]),
        (wg_hbm.at[own_head, :, part], wg_own),
        (wu_hbm.at[own_head, :, part], wu_own),
        (v_hbm.at[:, own_cols], kv.at[0, 1]),
        (r_hbm, rates.at[0]),
        (wd_hbm.at[own_head, part], wd_own),
        (q_hbm, q_ref),
        (wg_hbm, wg),
        (wu_hbm, wu),
        (wd_hbm, wd),
    ]
    barrier = pltpu.get_barrier_semaphore()
    peers = [along_x(d) for d in (1, -1)]
    peers += [along_z(d) for d in (1, -1, 2, -2)]
    for peer in peers:
        pl.semaphore_signal(barrier, inc=1, device_id={"seq": peer}, device_id_type=MESH)
    copies = [pltpu.make_async_copy(a, b, loads.at[i]) for i, (a, b) in enumerate(copies)]
    for copy in copies:
        copy.start()

    def start_z(g):
        def chunk(d):
            return own[g, :, rows(d)]

        for j, t in enumerate(STEPS):
            for i in range(3):
                near[g, 3 * j + i] = chunk(t + STRIDE * (i - 1))
            send(near.at[g, pl.ds(3 * j, 3)], got.at[g, pl.ds(3 * j, 3)], NEAR, g, along_z(t))
        near[g, 12] = chunk(-8)
        send(near.at[g, 12], got.at[g, 12], NEAR, g, along_z(-3))
        for i in range(3):
            near[g, 13 + i] = chunk(STRIDE * (i - 1))

    def collect(g):
        arrived(got.at[g], NEAR, g)
        for i in (0, 2, 1):
            total = near[g, 13 + i].astype(F32)
            for j in range(4):
                total = total + got[g, 3 * j + i].astype(F32)
            if i == 0:
                total = total + got[g, 12].astype(F32)
            near[g, 13 + i] = total.astype(BF16)
        send(near.at[g, pl.ds(14, 2)], far.at[g, pl.ds(0, 2)], FAR, g, along_z(STRIDE))
        send(near.at[g, pl.ds(13, 2)], far.at[g, pl.ds(2, 2)], FAR, g, along_z(-STRIDE))
        send(near.at[g, 13], far.at[g, 4], FAR, g, along_z(-2 * STRIDE))
        send(near.at[g, 15], far.at[g, 5], FAR, g, along_z(2 * STRIDE))

    def fill(g):
        arrived(far.at[g], FAR, g)
        parts = ((far[g, 5], far[g, 0], near[g, 13]), (far[g, 1], near[g, 14], far[g, 2]))
        parts += ((near[g, 15], far[g, 3], far[g, 4]),)
        for i, (a, b, c) in enumerate(parts):
            spread[g, i] = (a.astype(F32) + b.astype(F32) + c.astype(F32)).astype(BF16)
        for j, t in enumerate(STEPS):
            mine = spread.at[g, pl.ds(0, 3)]
            send(mine, spread.at[g, pl.ds(3 + 3 * j, 3)], FILL, g, along_z(t))
        send(spread.at[g, 0], spread.at[g, 15], FILL, g, along_z(3))

    def side(g):
        arrived(got.at[g], FILL, g)
        for j, t in enumerate((0,) + STEPS):
            for i in range(3):
                o_ref[g, x, :, rows(STRIDE * (i - 1) - t)] = spread[g, 3 * j + i]
        o_ref[g, x, :, rows(8)] = spread[g, 15]
        for d in (1, -1):
            send(o_ref.at[g, x], o_ref.at[g, x], SIDE, g, along_x(d))

    def pass_on(g):
        arrived(o_ref.at[g, pl.ds(0, 2)], SIDE, g)
        for origin, at, d in ((left_x, 0, 1), (right, dh // 2, -1)):
            piece = o_ref.at[g, origin, :, pl.ds(at, dh // 2)]
            send(piece, piece, PASS, g, along_x(d))

    def end(g):
        arrived(o_ref.at[g, 0], PASS, g)

    pl.semaphore_wait(barrier, len(peers))
    def tell(at, distance):
        for d in (distance, -distance):
            pl.semaphore_signal(
                beyond.at[at], inc=1, device_id={"seq": along_z(d)}, device_id_type=MESH
            )

    tell(0, 2)
    for i, (array, d) in enumerate(((k_hbm, 1), (v_hbm, -1))):
        send(array.at[:, own_cols], relay.at[i], RELAY, i, along_x(d))
    send(r_hbm, rates.at[1], RATES, 1, along_x(1))
    send(r_hbm, rates.at[3], RATES, 3, along_x(-1))
    for i, array in enumerate((k_hbm, v_hbm)):
        for d in (1, 3):
            send(array.at[:, other_cols], kv.at[d, i], TOKENS, d, along_x(d))
    for copy in copies[:6]:
        copy.wait()
    weights = (wg_own[...], wu_own[...], wd_own[...], s1, s2)

    def grads_from(d):
        rate = jnp.transpose(rates[d])
        rate = jnp.where(own_head == 0, rate[:, 0:1], rate[:, 1:2])
        vr = (rate * kv[d, 1].astype(F32)).astype(BF16)
        return enumerate(token_grads(kv[d, 0], vr, *weights))

    for i, grad in grads_from(0):
        acc[i] = grad
    for copy in copies[6:]:
        copy.wait()
    for h in range(heads):
        cols = slice(h * dh, (h + 1) * dh)
        app_ref[:, cols] = head_apply(h, q_ref[:, cols], wg, wu, wd)
    arrived(rates.at[1], RATES, 1)
    send(rates.at[1], rates.at[2], RATES, 2, along_x(1))
    for i, d in ((0, 1), (1, -1)):
        arrived(relay.at[i], RELAY, i)
        send(relay.at[i], kv.at[2, i], TOKENS, 2, along_x(d))
    arrived(rates.at[3], RATES, 3)
    for d in (1, 3):
        arrived(kv.at[d], TOKENS, d)
        for i, grad in grads_from(d):
            acc[i] = acc[i] + grad
    pl.semaphore_wait(beyond.at[0], 2)
    tell(1, 3)
    arrived(rates.at[2], RATES, 2)
    arrived(kv.at[2], TOKENS, 2)
    for i, grad in grads_from(2):
        total = (acc[i] + grad).astype(BF16)
        for c in range(2):
            own[divmod(2 * i + c, PER)] = total[:, c * 128 : (c + 1) * 128]
            if (2 * i + c + 1) % PER == 0:
                start_z((2 * i + c) // PER)
    pl.semaphore_wait(beyond.at[1], 2)
    stages = (collect, fill, side, pass_on)
    for stage in stages:
        for g in range(GROUPS):
            stage(g)
    early = begun_ref.shape[0]
    ready = GROUPS * early // (3 * heads)
    for g in range(ready):
        end(g)
    where = [(h, kind) for kind in ORDER for h in range(heads)]
    scales = [newton_start(o_ref, begun_ref, m, *where[m], heads) for m in range(early)]
    for s in range(HEAD_START):
        for _ in newton_step(begun_ref, a_ref, range(early), s, scales):
            pass
    for g in range(ready, GROUPS):
        end(g)
    for i in range(2):
        left(relay.at[i], RELAY, i)
    for d in range(1, NX):
        left(kv.at[d], TOKENS, d)
        left(rates.at[d], RATES, d)
    for g in range(GROUPS):
        left(got.at[g], NEAR, g)
        left(far.at[g], FAR, g)
        left(got.at[g], FILL, g)
        left(o_ref.at[g, pl.ds(0, 2)], SIDE, g)
        left(o_ref.at[g, 0], PASS, g)


def newton_start(t_ref, x_ref, m, h, kind, heads):
    blocks = []
    for c in range(NX):
        group, place = divmod(2 * ((kind + 1) % 3) + c % 2, PER)
        blocks.append(t_ref[group, heads * (c // 2) + h, place].astype(F32))
    total = jnp.concatenate(blocks, axis=1)
    x_ref[m] = total.astype(BF16)
    return 1.0 / (jnp.sqrt(jnp.sum(total * total, keepdims=True)) + 1e-07)


def newton_step(x_ref, a_ref, mats, s, scales):
    for m in mats:
        x = x_ref[m]
        square = dot(x, x, 1, 1)
        if s == 0:
            square = square * scales[m] * scales[m]
        a_ref[m] = square.astype(BF16)
    for m in mats:
        a = a_ref[m]
        a_ref[m] = (-4.775 * a.astype(F32) + 2.0315 * dot(a, a, 1, 0)).astype(BF16)
    for m in mats:
        x = x_ref[m]
        nxt = 3.4445 * x.astype(F32) + dot(a_ref[m], x, 1, 0)
        if s == 0:
            nxt = nxt * scales[m]
        if s == NS_STEPS - 1:
            nxt = nxt * (0.2 * math.sqrt(x.shape[1]))
        x_ref[m] = nxt.astype(BF16)
        yield m


def newton_kernel(
    t_ref, begun_ref, applied_ref, applied_hbm, gate_hbm, up_hbm, down_hbm, x_ref, a_ref, sems
):
    outs = (gate_hbm, up_hbm, down_hbm)
    heads = gate_hbm.shape[0]
    handed = pltpu.make_async_copy(applied_ref, applied_hbm, sems.at[heads * 3])
    handed.start()
    where = [(h, kind) for kind in ORDER for h in range(heads)]
    early = begun_ref.shape[0]
    scales = {}
    for m in range(early, len(where)):
        scales[m] = newton_start(t_ref, x_ref, m, *where[m], heads)
    for s in range(NS_STEPS):
        mats = range(early, len(where))
        if s >= HEAD_START:
            mats = range(len(where))
        if s == HEAD_START:
            x_ref[pl.ds(0, early)] = begun_ref[...]
        for m in newton_step(x_ref, a_ref, mats, s, scales):
            if s == NS_STEPS - 1:
                h, kind = where[m]
                pltpu.make_async_copy(x_ref.at[m], outs[kind].at[h], sems.at[m]).start()
    for m, (h, kind) in enumerate(where):
        pltpu.make_async_copy(x_ref.at[m], outs[kind].at[h], sems.at[m]).wait()
    handed.wait()


def per_device(queries, keys, values, token_rates, w_gate, w_up, w_down):
    heads, dh, hid = w_gate.shape
    tokens = queries.shape[0]
    vmem = pl.BlockSpec(memory_space=pltpu.VMEM)
    hbm = pl.BlockSpec(memory_space=pltpu.HBM)
    tile = (dh // NZ, hid // NX)
    half = hid * heads // NX
    travel = jax.ShapeDtypeStruct((GROUPS, NX, PER, dh, hid // NX), BF16)
    out = jax.ShapeDtypeStruct((tokens, heads * dh), BF16)
    weights = jax.ShapeDtypeStruct((heads, dh, hid), BF16)
    given = (queries, keys, values, token_rates, w_gate, w_up, w_down)
    given = [pltpu.with_memory_space_constraint(a, pltpu.HBM) for a in given]
    begun = jax.ShapeDtypeStruct((heads * 2, dh, hid), BF16)
    applied, total, begun = pl.pallas_call(
        main_kernel,
        name="grads_and_sum",
        out_shape=(out, travel, begun),
        in_specs=[hbm] * 7,
        out_specs=(vmem,) * 3,
        scratch_shapes=[
            pltpu.VMEM(queries.shape, BF16),
            pltpu.VMEM(w_gate.shape, BF16),
            pltpu.VMEM(w_up.shape, BF16),
            pltpu.VMEM(w_down.shape, BF16),
            pltpu.VMEM((dh, half), BF16),
            pltpu.VMEM((dh, half), BF16),
            pltpu.VMEM((half, dh), BF16),
            pltpu.VMEM((NX, 2, tokens, dh), BF16),
            pltpu.VMEM((NX,) + token_rates.shape, F32),
            pltpu.VMEM((3, dh, half), F32),
            pltpu.VMEM((GROUPS, PER, dh, hid // NX), BF16),
            pltpu.VMEM((2, tokens, dh), BF16),
            pltpu.VMEM((GROUPS, 16, PER) + tile, BF16),
            pltpu.VMEM((GROUPS, 13, PER) + tile, BF16),
            pltpu.VMEM((GROUPS, 6, PER) + tile, BF16),
            pltpu.VMEM((GROUPS, 16, PER) + tile, BF16),
            pltpu.VMEM((heads * 2, dh, dh), BF16),
            pltpu.SemaphoreType.DMA((10,)),
            pltpu.SemaphoreType.DMA((2 * KINDS, SLOTS)),
            pltpu.SemaphoreType.REGULAR((2,)),
        ],
        compiler_params=pltpu.CompilerParams(
            collective_id=0, has_side_effects=True, vmem_limit_bytes=32 << 20
        ),
    )(*given)
    return pl.pallas_call(
        newton_kernel,
        name="newton",
        out_shape=(out, weights, weights, weights),
        in_specs=[vmem] * 3,
        out_specs=(hbm,) * 4,
        scratch_shapes=[
            pltpu.VMEM((heads * 3, dh, hid), BF16),
            pltpu.VMEM((heads * 3, dh, dh), BF16),
            pltpu.SemaphoreType.DMA((heads * 3 + 1,)),
        ],
        compiler_params=pltpu.CompilerParams(vmem_limit_bytes=24 << 20),
    )(total, begun, applied)


def solution(mesh):
    in_specs = (
        P("seq", "head"),
        P("seq", "head"),
        P("seq", "head"),
        P("head", "seq"),
        P("head", None, None),
        P("head", None, None),
        P("head", None, None),
    )
    out_specs = (
        P("seq", "head"),
        P("head", None, None),
        P("head", None, None),
        P("head", None, None),
    )
    return jax.shard_map(
        per_device, mesh=mesh, in_specs=in_specs, out_specs=out_specs, check_vma=False
    )
```
